512 devices in a mesh: sec: 32 (over z, core), term: 16 (over y, x).
Axes of the slice: x: 4, y: 4, z: 16, core: 2. Of those that a mesh axis runs over, the one named last changes fastest.
Arguments:
- psi: bfloat16 [128, 4, 256, 256], P('sec'), may hold values from -6 to 6
- left_env: bfloat16 [64, 128, 256, 256], P('term', 'sec'), may hold values from -0.046875 to 0.046875
- right_env: bfloat16 [64, 256, 256], P('term'), may hold values from -0.375 to 0.375
- site_ops: float32 [64, 4, 4], P('term'), may hold values from -3 to 3
- coupling: int32 [64, 128], P('term', 'sec'), may hold values from -1 to 127, as said below
- live: int32 [128], P('sec'), may hold values from 128 to 256, as said below
Outputs:
- sigma: bfloat16 [128, 4, 256, 256], P('sec', None, 'term')
The draws below stay inside these ranges and needn't reach their ends.
Inputs may be any that keep to these rules, and one draw needn't show every extreme that they name: coupling[t, s] is -1 or a block within 2 of s; some terms couple at distance 2 in both directions. live sizes are at least 128.
All inputs are finite; a program needn't handle non-finite values.
Results may differ from the reference program's by a relative error of at most 0.018.
Values may be sent and summed in bfloat16 or wider, within the bound.
A program may use at most 64 MiB of HBM per device.

```python
import jax
import jax.numpy as jnp
from jax import lax

B = 256
K = 4
NS = 128
TERMS = 64


def draw_coupling(key, part):
    shift_key = jax.random.fold_in(key, 11)
    keep_key = jax.random.fold_in(key, 12)
    shifts = jax.random.randint(shift_key, (TERMS,), -2, 3)
    shifts = shifts.at[0].set(2)
    shifts = shifts.at[1].set(-2)
    target = jnp.arange(NS, dtype=jnp.int32)[None, :] + shifts[:, None]
    keeper = jax.random.randint(keep_key, (TERMS, NS), 0, 5) > 0
    valid = (target >= 0) & (target < NS) & keeper
    return jnp.where(valid, target, -1).astype(jnp.int32)


def draw_live(key, part):
    sizes = jax.random.randint(jax.random.fold_in(key, 21), (NS,), B // 2, B + 1)
    return sizes.at[0].set(B).astype(jnp.int32)


def shard_levels(own_key, extent, pieces, low, high):
    level = 1.0
    for axis_at, parts in pieces:
        draws = jax.random.uniform(jax.random.fold_in(jax.random.fold_in(own_key, 6), axis_at), (parts,), jnp.float32, low / len(pieces), high / len(pieces))
        level = level * jnp.repeat(jnp.exp(draws), extent[axis_at] // parts).reshape((-1,) + (1,) * (len(extent) - 1 - axis_at))
    return level


def gaussian(rng, extent, deviation, reach, pieces=(), kind=jnp.bfloat16):
    gain = shard_levels(rng, extent, pieces, -0.22, 0.18) if pieces else 1.0
    values = jax.random.normal(rng, extent, jnp.float32) * deviation * gain
    return jnp.minimum(jnp.maximum(values, -reach), reach).astype(kind)


def setup_inputs(seed: int = 0) -> dict:
    seeds = jax.random.split(jax.random.key(seed), 7)
    return {
        "psi": gaussian(seeds[0], (NS, K, B, B), 1.0, 6.0, ((0, 32),)),
        "left_env": gaussian(seeds[1], (TERMS, NS, B, B), (B * TERMS) ** -0.5, 0.046875, ((0, 16), (1, 32))),
        "right_env": gaussian(seeds[2], (TERMS, B, B), B ** -0.5, 0.375, ((0, 16),)),
        "site_ops": gaussian(seeds[3], (TERMS, K, K), K ** -0.5, 3.0, ((0, 16),), jnp.float32),
        "coupling": draw_coupling(jax.random.fold_in(seeds[6], 71), 0),
        "live": draw_live(jax.random.fold_in(seeds[6], 71), 0),
    }


def reference(psi, left_env, right_env, site_ops, coupling, live):
    width = psi.shape[2]

    def term_step(acc, inputs):
        left_t, right_t, ops_t, couple_t = inputs
        valid = couple_t >= 0
        index = jnp.where(valid, couple_t, 0).astype(jnp.int32)
        source = psi[index]
        mixed = jnp.einsum('kj,sjab->skab', ops_t.astype(jnp.float32), source.astype(jnp.float32))
        mixed = (mixed * valid[:, None, None, None].astype(jnp.float32)).astype(jnp.bfloat16)
        inner = jnp.einsum('sab,skbc->skac', left_t.astype(jnp.float32), mixed.astype(jnp.float32)).astype(jnp.bfloat16)
        outer = jnp.einsum('skac,cd->skad', inner.astype(jnp.float32), right_t.astype(jnp.float32))
        return acc + outer, None

    start = jnp.zeros(psi.shape, jnp.float32)
    total, unused = lax.scan(term_step, start, (left_env, right_env, site_ops, coupling))
    position = jnp.arange(width, dtype=jnp.int32)
    rows_ok = position[None, :] < live[:, None]
    keep = rows_ok[:, :, None] & rows_ok[:, None, :]
    result = jnp.where(keep[:, None, :, :], total, 0.0)
    return result.astype(jnp.bfloat16)
```

```python
import functools

import jax
import jax.numpy as jnp
from jax import lax
from jax.experimental import pallas as pl
from jax.experimental.pallas import tpu as pltpu
from jax.sharding import PartitionSpec as P

MESH = pl.DeviceIdType.MESH
SIDE = 4
GROUPS = ((1, 2), (0, 3))


def kernel(
    sections, chunk,
    psi, left, right, ops, coupling, out,
    mid, far, lcat, rbuf, ybuf, acc, relay1, direct1, comb1, red, relay2, direct2, comb2,
    local_sem, halo_send, halo_recv, send1, recv1, send2, recv2,
):
    sec = lax.axis_index("sec")
    term = lax.axis_index("term")
    x, y = term % SIDE, term // SIDE
    up, down = (sec + 1) % sections, (sec + sections - 1) % sections
    near = (
        (y * SIDE + (x + 1) % SIDE, y * SIDE + (x + SIDE - 1) % SIDE),
        ((y + 1) % SIDE * SIDE + x, (y + SIDE - 1) % SIDE * SIDE + x),
    )
    place = (x, y)

    local = []

    def fetch(src, dst):
        copy = pltpu.make_async_copy(src, dst, local_sem.at[len(local)])
        copy.start()
        local.append(copy)

    fetch(psi, mid.at[pl.ds(1, 4)])
    fetch(right, rbuf)
    for t in range(4):
        for s in range(4):
            fetch(left.at[t, s], lcat.at[s, :, pl.ds(256 * t, 256)])

    barrier = pltpu.get_barrier_semaphore()
    for other in (up, down):
        pl.semaphore_signal(barrier, inc=1, device_id={"sec": other, "term": term}, device_id_type=MESH)
    for pair in near:
        for other in pair:
            pl.semaphore_signal(barrier, inc=1, device_id={"sec": sec, "term": other}, device_id_type=MESH)
    pl.semaphore_wait(barrier, 6)

    def halo(n, src, dst, other):
        copy = pltpu.make_async_remote_copy(
            src_ref=src, dst_ref=dst, send_sem=halo_send.at[n], recv_sem=halo_recv.at[n],
            device_id={"sec": other, "term": term}, device_id_type=MESH,
        )
        copy.start()
        return copy

    halos = [
        halo(0, psi.at[3], mid.at[0], up),
        halo(1, psi.at[0], mid.at[5], down),
        halo(2, psi.at[2], far.at[0], up),
        halo(3, psi.at[1], far.at[1], down),
    ]

    def compute(g, i, s):
        def term_step(t, carry):
            target = coupling[t, s]
            valid = target >= 0
            place_in = target - sec * 4
            index = jnp.clip(place_in + 1, 0, 5)
            is_far = jnp.logical_or(place_in == -2, place_in == 5)
            coef = [[jnp.where(valid, ops[t, k, j], 0.0) for j in range(4)] for k in range(4)]
            weights = rbuf[t]
            for r in range(0, 256, chunk):
                rows = pl.ds(r, chunk)
                source = []
                for j in range(4):
                    value = mid[index, j, rows, :]
                    if g == 1:
                        value = jnp.where(is_far, far[i, j, rows, :], value)
                    source.append(value.astype(jnp.float32))
                mixed = []
                for k in range(4):
                    total = coef[k][0] * source[0]
                    for j in range(1, 4):
                        total = total + coef[k][j] * source[j]
                    mixed.append(total.astype(jnp.bfloat16))
                inner = jnp.dot(
                    jnp.concatenate(mixed, axis=0), weights, preferred_element_type=jnp.float32
                ).astype(jnp.bfloat16)
                for k in range(4):
                    ybuf[t, rows, pl.ds(256 * k, 256)] = inner[k * chunk : (k + 1) * chunk]
            return carry

        lax.fori_loop(0, 4, term_step, 0)

        lhs = lcat[s]
        for k in range(4):
            rhs = ybuf[:, :, pl.ds(256 * k, 256)].reshape(1024, 256)
            total = jnp.dot(lhs, rhs, preferred_element_type=jnp.float32)
            acc[g, i, k] = total.astype(jnp.bfloat16).reshape(SIDE, SIDE, 16, 256)

    pending = []

    def send(src, dst, send_sem, recv_sem, axis, direction):
        copy = pltpu.make_async_remote_copy(
            src_ref=src, dst_ref=dst, send_sem=send_sem, recv_sem=recv_sem,
            device_id={"sec": sec, "term": near[axis][direction]}, device_id_type=MESH,
        )
        copy.start()
        pending.append(copy)
        return copy

    def slab(g, h, d, at):
        if h == 0:
            return (g, slice(None), d, slice(None), at)
        return (g, slice(None), 2 + d, at)

    copies = {}

    def first(g, h):
        at = place[h]
        opposite = (at + 2) % SIDE
        sides = ((at + 1) % SIDE, (at + 3) % SIDE)
        for d in range(2):
            copies[1, g, h, 0, d] = send(
                acc.at[slab(g, h, d, opposite)], relay1.at[g, h, d], send1.at[g, h, 0, d], recv1.at[g, h, 0, d], h, d
            )
        for d in range(2):
            copies[1, g, h, 1, d] = send(
                acc.at[slab(g, h, 1 - d, sides[d])], direct1.at[g, h, d], send1.at[g, h, 1, d], recv1.at[g, h, 1, d], h, d
            )

    def first_pass_on(g, h):
        at = place[h]
        sides = ((at + 1) % SIDE, (at + 3) % SIDE)
        for d in range(2):
            copies[1, g, h, 0, d].wait_recv()
            own = acc[slab(g, h, d, sides[d])].astype(jnp.float32)
            relay1[g, h, d] = (relay1[g, h, d].astype(jnp.float32) + own).astype(jnp.bfloat16)
            copies[1, g, h, 2, d] = send(
                relay1.at[g, h, d], comb1.at[g, h, d], send1.at[g, h, 2, d], recv1.at[g, h, 2, d], h, d
            )

    def second(g, h):
        at = place[h]
        for d in range(2):
            copies[1, g, h, 1, 1 - d].wait_recv()
            copies[1, g, h, 2, d].wait_recv()
            own = acc[slab(g, h, d, at)].astype(jnp.float32)
            total = own + direct1[g, h, 1 - d].astype(jnp.float32) + comb1[g, h, d].astype(jnp.float32)
            red[g, h, d] = total.astype(jnp.bfloat16)
        axis = 1 - h
        at = place[axis]
        opposite = (at + 2) % SIDE
        sides = ((at + 1) % SIDE, (at + 3) % SIDE)
        for d in range(2):
            copies[2, g, h, 0, d] = send(
                red.at[g, h, d, :, opposite], relay2.at[g, h, d], send2.at[g, h, 0, d], recv2.at[g, h, 0, d], axis, d
            )
        for d in range(2):
            copies[2, g, h, 1, d] = send(
                red.at[g, h, 1 - d, :, sides[d]], direct2.at[g, h, d], send2.at[g, h, 1, d], recv2.at[g, h, 1, d], axis, d
            )

    def second_pass_on(g, h):
        axis = 1 - h
        at = place[axis]
        sides = ((at + 1) % SIDE, (at + 3) % SIDE)
        for d in range(2):
            copies[2, g, h, 0, d].wait_recv()
            own = red[g, h, d, :, sides[d]].astype(jnp.float32)
            relay2[g, h, d] = (relay2[g, h, d].astype(jnp.float32) + own).astype(jnp.bfloat16)
            copies[2, g, h, 2, d] = send(
                relay2.at[g, h, d], comb2.at[g, h, d], send2.at[g, h, 2, d], recv2.at[g, h, 2, d], axis, d
            )

    def finish(g, h):
        at = place[1 - h]
        for d in range(2):
            copies[2, g, h, 1, 1 - d].wait_recv()
            copies[2, g, h, 2, d].wait_recv()
            own = red[g, h, d, :, at].astype(jnp.float32)
            total = own + direct2[g, h, 1 - d].astype(jnp.float32) + comb2[g, h, d].astype(jnp.float32)
            for i in range(2):
                out[GROUPS[g][i], 2 * h + d] = total[i].astype(jnp.bfloat16)

    def both(step, g):
        for h in range(2):
            step(g, h)

    for copy in local:
        copy.wait()
    halos[0].wait_recv()
    halos[1].wait_recv()
    lax.fori_loop(0, 2, lambda i, c: (compute(0, i, 1 + i), c)[1], 0)
    both(first, 0)
    halos[2].wait_recv()
    halos[3].wait_recv()
    compute(1, 0, 0)
    both(first_pass_on, 0)
    compute(1, 1, 3)
    both(first, 1)
    both(second, 0)
    both(first_pass_on, 1)
    both(second_pass_on, 0)
    both(second, 1)
    both(finish, 0)
    both(second_pass_on, 1)
    both(finish, 1)
    for copy in halos + pending:
        copy.wait_send()


def on_device(psi, left_env, right_env, site_ops, coupling, live):
    sec_count, states, width, _ = psi.shape
    row_count = width // lax.axis_size("term")
    anywhere = pl.BlockSpec(memory_space=pl.ANY)
    scalars = pl.BlockSpec(memory_space=pltpu.SMEM)
    bf16 = jnp.bfloat16
    dma = pltpu.SemaphoreType.DMA
    mine = pl.pallas_call(
        functools.partial(kernel, lax.axis_size("sec"), 64),
        out_shape=jax.ShapeDtypeStruct((sec_count, states, row_count, width), bf16),
        in_specs=[anywhere, anywhere, anywhere, scalars, scalars],
        out_specs=pl.BlockSpec(memory_space=pltpu.VMEM),
        scratch_shapes=[
            pltpu.VMEM((6, 4, 256, 256), bf16),
            pltpu.VMEM((2, 4, 256, 256), bf16),
            pltpu.VMEM((4, 256, 1024), bf16),
            pltpu.VMEM((4, 256, 256), bf16),
            pltpu.VMEM((4, 256, 1024), bf16),
            pltpu.VMEM((2, 2, 4, SIDE, SIDE, 16, 256), bf16),
            pltpu.VMEM((2, 2, 2, 2, SIDE, 16, 256), bf16),
            pltpu.VMEM((2, 2, 2, 2, SIDE, 16, 256), bf16),
            pltpu.VMEM((2, 2, 2, 2, SIDE, 16, 256), bf16),
            pltpu.VMEM((2, 2, 2, 2, SIDE, 16, 256), bf16),
            pltpu.VMEM((2, 2, 2, 2, 16, 256), bf16),
            pltpu.VMEM((2, 2, 2, 2, 16, 256), bf16),
            pltpu.VMEM((2, 2, 2, 2, 16, 256), bf16),
            dma((18,)),
            dma((4,)),
            dma((4,)),
            dma((2, 2, 3, 2)),
            dma((2, 2, 3, 2)),
            dma((2, 2, 3, 2)),
            dma((2, 2, 3, 2)),
        ],
        compiler_params=pltpu.CompilerParams(
            collective_id=0, has_side_effects=True, vmem_limit_bytes=48 << 20
        ),
    )(psi, left_env, right_env, site_ops, coupling)
    rows_here = lax.axis_index("term") * row_count + jnp.arange(row_count, dtype=jnp.int32)
    columns = jnp.arange(width, dtype=jnp.int32)
    keep = (rows_here[None, :] < live[:, None])[:, :, None] & (columns[None, :] < live[:, None])[:, None, :]
    return jnp.where(keep[:, None, :, :], mine, jnp.zeros((), bf16))


def solution(mesh):
    placed = (
        P("sec", None, None, None),
        P("term", "sec", None, None),
        P("term", None, None),
        P("term", None, None),
        P("term", "sec"),
        P("sec"),
    )
    return jax.shard_map(
        on_device,
        mesh=mesh,
        in_specs=placed,
        out_specs=P("sec", None, "term", None),
        check_vma=False,
    )
```

```python
import functools

import jax
import jax.numpy as jnp
from jax import lax
from jax.experimental import pallas as pl
from jax.experimental.pallas import tpu as pltpu
from jax.sharding import PartitionSpec as P

MESH = pl.DeviceIdType.MESH
SIDE = 4
RINGS = (True, True, True, False)
CHUNK = 64


def kernel(
    sections,
    psi, left, right, ops, coupling, live, out,
    held, close, far, lcat, rbuf, ybuf, acc, relay, direct, comb, whole, red, parts,
    local_sem, halo_send, halo_recv, send1, recv1, send2, recv2,
):
    sec = lax.axis_index("sec")
    term = lax.axis_index("term")
    x, y = term % SIDE, term // SIDE
    core = sec % 2
    partner = sec + 1 - 2 * core
    distant = (sec + sections - 1 + 2 * core) % sections
    has_distant = jnp.logical_and(sec > 0, sec < sections - 1)

    def mirror(b):
        return b + core * (3 - 2 * b)

    near = (
        (y * SIDE + (x + 1) % SIDE, y * SIDE + (x + 3) % SIDE, y * SIDE + (x + 2) % SIDE),
        ((y + 1) % SIDE * SIDE + x, (y + 3) % SIDE * SIDE + x, (y + 2) % SIDE * SIDE + x),
    )
    place = (x, y)
    order = [mirror(b) for b in (2, 3, 1, 0)]

    def fetch(n, src, dst):
        copy = pltpu.make_async_copy(src, dst, local_sem.at[n])
        copy.start()
        return copy

    local = [fetch(0, psi, held.at[pl.ds(0, 4)]), fetch(1, right, rbuf)]
    lefts = [fetch(2 + c, left.at[:, order[c]], lcat.at[c]) for c in range(4)]

    def at_sec(other):
        return {"sec": other, "term": term}

    def at_term(other):
        return {"sec": sec, "term": other}

    barrier = pltpu.get_barrier_semaphore()
    pl.semaphore_signal(barrier, inc=1, device_id=at_sec(partner), device_id_type=MESH)

    @pl.when(has_distant)
    def _():
        pl.semaphore_signal(barrier, inc=1, device_id=at_sec(distant), device_id_type=MESH)

    for axis in range(2):
        for d in range(3):
            pl.semaphore_signal(barrier, inc=1, device_id=at_term(near[axis][d]), device_id_type=MESH)
    pl.semaphore_wait(barrier, 7 + has_distant.astype(jnp.int32))

    def halo(n, src, dst, other):
        return pltpu.make_async_remote_copy(
            src_ref=src, dst_ref=dst, send_sem=halo_send.at[n], recv_sem=halo_recv.at[n],
            device_id=at_sec(other), device_id_type=MESH,
        )

    halos = [
        halo(0, psi.at[mirror(0)], close, distant),
        halo(1, psi.at[mirror(1)], far, distant),
        halo(2, psi.at[mirror(3)], held.at[4], partner),
        halo(3, psi.at[mirror(2)], held.at[5], partner),
    ]

    @pl.when(has_distant)
    def _():
        halos[0].start()
        halos[1].start()

    halos[2].start()
    halos[3].start()

    def compute(c):
        s = order[c]
        for t in range(4):
            target = coupling[t, s]
            valid = target >= 0
            block = target - sec * 4
            seen = mirror(block)
            own = jnp.logical_and(block >= 0, block < 4)
            index = jnp.where(own, block, jnp.where(seen == 4, 4, 5))
            coef = [
                [jnp.where(valid, ops[t, k, j], 0.0).astype(jnp.bfloat16) for j in range(4)] for k in range(4)
            ]
            weights = rbuf[t]
            for r in range(0, 256, CHUNK):
                rows = pl.ds(r, CHUNK)
                source = []
                for j in range(4):
                    value = held[index, j, rows, :]
                    if c >= 2:
                        value = jnp.where(seen == -1, close[j, rows, :], value)
                    if c == 3:
                        value = jnp.where(seen == -2, far[j, rows, :], value)
                    source.append(value)
                mixed = []
                for k in range(4):
                    total = coef[k][0] * source[0]
                    for j in range(1, 4):
                        total = total + coef[k][j] * source[j]
                    mixed.append(total)
                inner = jnp.dot(
                    jnp.concatenate(mixed, axis=0), weights, preferred_element_type=jnp.float32
                ).astype(jnp.bfloat16)
                for k in range(4):
                    ybuf[t, rows, pl.ds(256 * k, 256)] = inner[k * CHUNK : (k + 1) * CHUNK]
        for k in range(4):
            total = None
            for t in range(4):
                term_part = jnp.dot(
                    lcat[c, t], ybuf[t, :, pl.ds(256 * k, 256)], preferred_element_type=jnp.float32
                )
                total = term_part if total is None else total + term_part
            acc[c, k] = total.astype(jnp.bfloat16).reshape(SIDE, SIDE, 16, 256)

    pending = []
    copies = {}

    def send(src, dst, send_sem, recv_sem, axis, direction):
        copy = pltpu.make_async_remote_copy(
            src_ref=src, dst_ref=dst, send_sem=send_sem, recv_sem=recv_sem,
            device_id=at_term(near[axis][direction]), device_id_type=MESH,
        )
        copy.start()
        pending.append(copy)
        return copy

    def targets(axis):
        at = place[axis]
        return ((at + 1) % SIDE, (at + 3) % SIDE, (at + 2) % SIDE)

    def slab(c, h, d, at):
        return (c, 2 * h + d, slice(None), at) if h == 0 else (c, 2 * h + d, at)

    def pair(c, h, at):
        return (c, pl.ds(2 * h, 2), slice(None), at) if h == 0 else (c, pl.ds(2 * h, 2), at)

    def first(c):
        for h in range(2):
            goal = targets(h)
            if RINGS[c]:
                for d in range(2):
                    copies[1, c, h, 0, d] = send(
                        acc.at[slab(c, h, d, goal[2])], relay.at[c, h, d],
                        send1.at[c, h, 0, d], recv1.at[c, h, 0, d], h, d,
                    )
                for d in range(2):
                    copies[1, c, h, 1, d] = send(
                        acc.at[slab(c, h, 1 - d, goal[d])], direct.at[c, h, d],
                        send1.at[c, h, 1, d], recv1.at[c, h, 1, d], h, d,
                    )
            else:
                for d in (2, 0, 1):
                    copies[1, c, h, d] = send(
                        acc.at[pair(c, h, goal[d])], whole.at[h, d],
                        send1.at[c, h, d, 0], recv1.at[c, h, d, 0], h, d,
                    )

    def pass_on(c):
        for h in range(2):
            goal = targets(h)
            for d in range(2):
                copies[1, c, h, 0, d].wait_recv()
                own = acc[slab(c, h, d, goal[d])].astype(jnp.float32)
                relay[c, h, d] = (relay[c, h, d].astype(jnp.float32) + own).astype(jnp.bfloat16)
                copies[1, c, h, 2, d] = send(
                    relay.at[c, h, d], comb.at[c, h, d], send1.at[c, h, 2, d], recv1.at[c, h, 2, d], h, d
                )

    def second(c):
        for h in range(2):
            if RINGS[c]:
                for d in range(2):
                    copies[1, c, h, 1, 1 - d].wait_recv()
                    copies[1, c, h, 2, d].wait_recv()
                    total = acc[slab(c, h, d, place[h])].astype(jnp.float32)
                    total = total + direct[c, h, 1 - d].astype(jnp.float32) + comb[c, h, d].astype(jnp.float32)
                    red[c, h, d] = total.astype(jnp.bfloat16)
            else:
                total = acc[pair(c, h, place[h])].astype(jnp.float32)
                for d in range(3):
                    copies[1, c, h, d].wait_recv()
                    total = total + whole[h, d].astype(jnp.float32)
                red[c, h] = total.astype(jnp.bfloat16)
            goal = targets(1 - h)
            for d in (2, 0, 1):
                copies[2, c, h, d] = send(
                    red.at[c, h, :, goal[d]], parts.at[c, h, d], send2.at[c, h, d], recv2.at[c, h, d], 1 - h, d
                )

    row = term * 16 + lax.broadcasted_iota(jnp.int32, (2, 16, 256), 1)
    column = lax.broadcasted_iota(jnp.int32, (2, 16, 256), 2)
    furthest = jnp.maximum(row, column)

    def finish(c):
        s = order[c]
        for h in range(2):
            total = red[c, h, :, place[1 - h]].astype(jnp.float32)
            for d in range(3):
                copies[2, c, h, d].wait_recv()
                total = total + parts[c, h, d].astype(jnp.float32)
            out[s, pl.ds(2 * h, 2)] = jnp.where(furthest < live[s], total, 0.0).astype(jnp.bfloat16)

    for copy in local:
        copy.wait()
    halos[2].wait_recv()
    halos[3].wait_recv()
    lefts[0].wait()
    compute(0)
    first(0)
    lefts[1].wait()
    compute(1)
    first(1)
    pass_on(0)

    @pl.when(has_distant)
    def _():
        halos[0].wait_recv()

    lefts[2].wait()
    compute(2)
    first(2)
    pass_on(1)
    second(0)
    pass_on(2)
    second(1)

    @pl.when(has_distant)
    def _():
        halos[1].wait_recv()

    lefts[3].wait()
    compute(3)
    first(3)
    second(2)
    finish(0)
    finish(1)
    second(3)
    finish(2)
    finish(3)

    @pl.when(has_distant)
    def _():
        halos[0].wait_send()
        halos[1].wait_send()

    for copy in halos[2:] + pending:
        copy.wait_send()


def on_device(psi, left_env, right_env, site_ops, coupling, live):
    sec_count, states, width, _ = psi.shape
    row_count = width // lax.axis_size("term")
    anywhere = pl.BlockSpec(memory_space=pl.ANY)
    scalars = pl.BlockSpec(memory_space=pltpu.SMEM)
    bf16 = jnp.bfloat16
    dma = pltpu.SemaphoreType.DMA
    return pl.pallas_call(
        functools.partial(kernel, lax.axis_size("sec")),
        out_shape=jax.ShapeDtypeStruct((sec_count, states, row_count, width), bf16),
        in_specs=[anywhere, anywhere, anywhere, scalars, scalars, scalars],
        out_specs=pl.BlockSpec(memory_space=pltpu.VMEM),
        scratch_shapes=[
            pltpu.VMEM((6, 4, 256, 256), bf16),
            pltpu.VMEM((4, 256, 256), bf16),
            pltpu.VMEM((4, 256, 256), bf16),
            pltpu.VMEM((4, 4, 256, 256), bf16),
            pltpu.VMEM((4, 256, 256), bf16),
            pltpu.VMEM((4, 256, 1024), bf16),
            pltpu.VMEM((4, 4, SIDE, SIDE, 16, 256), bf16),
            pltpu.VMEM((4, 2, 2, SIDE, 16, 256), bf16),
            pltpu.VMEM((4, 2, 2, SIDE, 16, 256), bf16),
            pltpu.VMEM((4, 2, 2, SIDE, 16, 256), bf16),
            pltpu.VMEM((2, 3, 2, SIDE, 16, 256), bf16),
            pltpu.VMEM((4, 2, 2, SIDE, 16, 256), bf16),
            pltpu.VMEM((4, 2, 3, 2, 16, 256), bf16),
            dma((6,)),
            dma((4,)),
            dma((4,)),
            dma((4, 2, 3, 2)),
            dma((4, 2, 3, 2)),
            dma((4, 2, 3)),
            dma((4, 2, 3)),
        ],
        compiler_params=pltpu.CompilerParams(
            collective_id=0, has_side_effects=True, vmem_limit_bytes=63 << 20
        ),
    )(psi, left_env, right_env, site_ops, coupling, live)


def solution(mesh):
    placed = (
        P("sec", None, None, None),
        P("term", "sec", None, None),
        P("term", None, None),
        P("term", None, None),
        P("term", "sec"),
        P("sec"),
    )
    return jax.shard_map(
        on_device,
        mesh=mesh,
        in_specs=placed,
        out_specs=P("sec", None, "term", None),
        check_vma=False,
    )
```

```python
import functools

import jax
import jax.numpy as jnp
from jax import lax
from jax.experimental import pallas as pl
from jax.experimental.pallas import tpu as pltpu
from jax.sharding import PartitionSpec as P

MESH = pl.DeviceIdType.MESH
SIDE = 4
CHUNK = 64


def kernel(
    sections,
    psi, left, right, ops, coupling, live, out,
    held, after, close, far, lcat, rbuf, ybuf, acc, relay, direct, comb, red, parts,
    local_sem, halo_send, halo_recv, share_send, share_recv, send1, recv1, send2, recv2,
):
    sec = lax.axis_index("sec")
    term = lax.axis_index("term")
    x, y = term % SIDE, term // SIDE
    core = sec % 2
    partner = sec + 1 - 2 * core
    distant = (sec + sections - 1 + 2 * core) % sections
    has_distant = jnp.logical_and(sec > 0, sec < sections - 1)

    def mirror(b):
        return b + core * (3 - 2 * b)

    near = (
        (y * SIDE + (x + 1) % SIDE, y * SIDE + (x + 3) % SIDE, y * SIDE + (x + 2) % SIDE),
        ((y + 1) % SIDE * SIDE + x, (y + 3) % SIDE * SIDE + x, (y + 2) % SIDE * SIDE + x),
    )
    place = (x, y)
    order = [mirror(b) for b in (2, 3, 1, 0)]

    def fetch(n, src, dst):
        copy = pltpu.make_async_copy(src, dst, local_sem.at[n])
        copy.start()
        return copy

    local = [fetch(0, psi, held.at[pl.ds(0, 4)]), fetch(1, right, rbuf)]
    lefts = [fetch(2 + c, left.at[:, order[c]], lcat.at[c]) for c in range(4)]

    def at_sec(other):
        return {"sec": other, "term": term}

    def at_term(other):
        return {"sec": sec, "term": other}

    barrier = pltpu.get_barrier_semaphore()
    pl.semaphore_signal(barrier, inc=1, device_id=at_sec(partner), device_id_type=MESH)

    @pl.when(has_distant)
    def _():
        pl.semaphore_signal(barrier, inc=1, device_id=at_sec(distant), device_id_type=MESH)

    for axis in range(2):
        for d in range(3):
            pl.semaphore_signal(barrier, inc=1, device_id=at_term(near[axis][d]), device_id_type=MESH)
    pl.semaphore_wait(barrier, 7 + has_distant.astype(jnp.int32))

    def halo(n, src, dst, other):
        return pltpu.make_async_remote_copy(
            src_ref=src, dst_ref=dst, send_sem=halo_send.at[n], recv_sem=halo_recv.at[n],
            device_id=at_sec(other), device_id_type=MESH,
        )

    mine = x + core * (y - x)
    theirs = y + core * (x - y)
    halos = [
        halo(0, psi.at[mirror(1), theirs], far.at[theirs], distant),
        halo(1, psi.at[mirror(0)], close, distant),
        halo(2, psi.at[mirror(3)], held.at[4], partner),
        halo(3, psi.at[mirror(2)], after, partner),
    ]
    shares = [
        pltpu.make_async_remote_copy(
            src_ref=far.at[mine], dst_ref=far.at[mine], send_sem=share_send.at[d], recv_sem=share_recv.at[d],
            device_id=at_term(near[0][d] + core * (near[1][d] - near[0][d])), device_id_type=MESH,
        )
        for d in range(3)
    ]

    @pl.when(has_distant)
    def _():
        halos[0].start()
        halos[1].start()

    halos[2].start()
    halos[3].start()

    def compute(c):
        s = order[c]
        for t in range(4):
            target = coupling[t, s]
            valid = target >= 0
            block = jnp.where(valid, target - sec * 4, 0)
            seen = mirror(block)
            own = jnp.logical_and(block >= 0, block < 4)
            index = jnp.where(own, block, 4)
            coef = [
                [jnp.where(valid, ops[t, k, j], 0.0).astype(jnp.bfloat16) for j in range(4)] for k in range(4)
            ]
            weights = rbuf[t]
            for r in range(0, 256, CHUNK):
                rows = pl.ds(r, CHUNK)
                source = []
                for j in range(4):
                    value = held[index, j, rows, :]
                    if c == 1:
                        value = jnp.where(seen == 5, after[j, rows, :], value)
                    if c >= 2:
                        value = jnp.where(seen == -1, close[j, rows, :], value)
                    if c == 3:
                        value = jnp.where(seen == -2, far[j, rows, :], value)
                    source.append(value)
                mixed = []
                for k in range(4):
                    total = coef[k][0] * source[0]
                    for j in range(1, 4):
                        total = total + coef[k][j] * source[j]
                    mixed.append(total)
                inner = jnp.dot(
                    jnp.concatenate(mixed, axis=0), weights, preferred_element_type=jnp.float32
                ).astype(jnp.bfloat16)
                for k in range(4):
                    ybuf[t, rows, pl.ds(256 * k, 256)] = inner[k * CHUNK : (k + 1) * CHUNK]
        for k in range(4):
            total = None
            for t in range(4):
                term_part = jnp.dot(
                    lcat[c, t], ybuf[t, :, pl.ds(256 * k, 256)], preferred_element_type=jnp.float32
                )
                total = term_part if total is None else total + term_part
            acc[c, k] = total.astype(jnp.bfloat16).reshape(SIDE, SIDE, 16, 256)

    pending = []
    copies = {}

    def send(src, dst, send_sem, recv_sem, axis, direction):
        copy = pltpu.make_async_remote_copy(
            src_ref=src, dst_ref=dst, send_sem=send_sem, recv_sem=recv_sem,
            device_id=at_term(near[axis][direction]), device_id_type=MESH,
        )
        copy.start()
        pending.append(copy)
        return copy

    def targets(axis):
        at = place[axis]
        return ((at + 1) % SIDE, (at + 3) % SIDE, (at + 2) % SIDE)

    def slab(c, h, d, at):
        return (c, 2 * h + d, slice(None), at) if h == 0 else (c, 2 * h + d, at)

    def first(c):
        for h in range(2):
            goal = targets(h)
            for d in range(2):
                copies[1, c, h, 0, d] = send(
                    acc.at[slab(c, h, d, goal[2])], relay.at[c, h, d],
                    send1.at[c, h, 0, d], recv1.at[c, h, 0, d], h, d,
                )
            for d in range(2):
                copies[1, c, h, 1, d] = send(
                    acc.at[slab(c, h, 1 - d, goal[d])], direct.at[c, h, d],
                    send1.at[c, h, 1, d], recv1.at[c, h, 1, d], h, d,
                )

    def pass_on(c):
        for h in range(2):
            goal = targets(h)
            for d in range(2):
                copies[1, c, h, 0, d].wait_recv()
                own = acc[slab(c, h, d, goal[d])].astype(jnp.float32)
                relay[c, h, d] = (relay[c, h, d].astype(jnp.float32) + own).astype(jnp.bfloat16)
                copies[1, c, h, 2, d] = send(
                    relay.at[c, h, d], comb.at[c, h, d], send1.at[c, h, 2, d], recv1.at[c, h, 2, d], h, d
                )

    def second(c):
        for h in range(2):
            for d in range(2):
                copies[1, c, h, 1, 1 - d].wait_recv()
                copies[1, c, h, 2, d].wait_recv()
                total = acc[slab(c, h, d, place[h])].astype(jnp.float32)
                total = total + direct[c, h, 1 - d].astype(jnp.float32) + comb[c, h, d].astype(jnp.float32)
                red[c, h, d] = total.astype(jnp.bfloat16)
            goal = targets(1 - h)
            for d in (2, 0, 1):
                copies[2, c, h, d] = send(
                    red.at[c, h, :, goal[d]], parts.at[c, h, d], send2.at[c, h, d], recv2.at[c, h, d], 1 - h, d
                )

    row = term * 16 + lax.broadcasted_iota(jnp.int32, (2, 16, 256), 1)
    column = lax.broadcasted_iota(jnp.int32, (2, 16, 256), 2)
    furthest = jnp.maximum(row, column)

    def finish(c):
        s = order[c]
        for h in range(2):
            total = red[c, h, :, place[1 - h]].astype(jnp.float32)
            for d in range(3):
                copies[2, c, h, d].wait_recv()
                total = total + parts[c, h, d].astype(jnp.float32)
            out[s, pl.ds(2 * h, 2)] = jnp.where(furthest < live[s], total, 0.0).astype(jnp.bfloat16)

    for copy in local:
        copy.wait()
    halos[2].wait_recv()

    @pl.when(has_distant)
    def _():
        halos[0].wait_recv()
        for copy in shares:
            copy.start()

    lefts[0].wait()
    compute(0)
    first(0)
    lefts[1].wait()
    halos[3].wait_recv()
    compute(1)
    first(1)

    @pl.when(has_distant)
    def _():
        halos[1].wait_recv()

    lefts[2].wait()
    compute(2)
    first(2)
    pass_on(0)
    pass_on(1)

    @pl.when(has_distant)
    def _():
        for copy in shares:
            copy.wait_recv()

    lefts[3].wait()
    compute(3)
    first(3)
    pass_on(2)
    pass_on(3)
    second(0)
    second(1)
    second(2)
    second(3)
    finish(0)
    finish(1)
    finish(2)
    finish(3)

    @pl.when(has_distant)
    def _():
        for copy in halos[:2] + shares:
            copy.wait_send()

    for copy in halos[2:] + pending:
        copy.wait_send()


def on_device(psi, left_env, right_env, site_ops, coupling, live):
    sec_count, states, width, _ = psi.shape
    row_count = width // lax.axis_size("term")
    anywhere = pl.BlockSpec(memory_space=pl.ANY)
    scalars = pl.BlockSpec(memory_space=pltpu.SMEM)
    bf16 = jnp.bfloat16
    dma = pltpu.SemaphoreType.DMA
    return pl.pallas_call(
        functools.partial(kernel, lax.axis_size("sec")),
        out_shape=jax.ShapeDtypeStruct((sec_count, states, row_count, width), bf16),
        in_specs=[anywhere, anywhere, anywhere, scalars, scalars, scalars],
        out_specs=pl.BlockSpec(memory_space=pltpu.VMEM),
        scratch_shapes=[
            pltpu.VMEM((5, 4, 256, 256), bf16),
            pltpu.VMEM((4, 256, 256), bf16),
            pltpu.VMEM((4, 256, 256), bf16),
            pltpu.VMEM((4, 256, 256), bf16),
            pltpu.VMEM((4, 4, 256, 256), bf16),
            pltpu.VMEM((4, 256, 256), bf16),
            pltpu.VMEM((4, 256, 1024), bf16),
            pltpu.VMEM((4, 4, SIDE, SIDE, 16, 256), bf16),
            pltpu.VMEM((4, 2, 2, SIDE, 16, 256), bf16),
            pltpu.VMEM((4, 2, 2, SIDE, 16, 256), bf16),
            pltpu.VMEM((4, 2, 2, SIDE, 16, 256), bf16),
            pltpu.VMEM((4, 2, 2, SIDE, 16, 256), bf16),
            pltpu.VMEM((4, 2, 3, 2, 16, 256), bf16),
            dma((6,)),
            dma((4,)),
            dma((4,)),
            dma((3,)),
            dma((3,)),
            dma((4, 2, 3, 2)),
            dma((4, 2, 3, 2)),
            dma((4, 2, 3)),
            dma((4, 2, 3)),
        ],
        compiler_params=pltpu.CompilerParams(
            collective_id=0, has_side_effects=True, vmem_limit_bytes=63 << 20
        ),
    )(psi, left_env, right_env, site_ops, coupling, live)


def solution(mesh):
    placed = (
        P("sec", None, None, None),
        P("term", "sec", None, None),
        P("term", None, None),
        P("term", None, None),
        P("term", "sec"),
        P("sec"),
    )
    return jax.shard_map(
        on_device,
        mesh=mesh,
        in_specs=placed,
        out_specs=P("sec", None, "term", None),
        check_vma=False,
    )
```

```python
import functools

import jax
import jax.numpy as jnp
from jax import lax
from jax.experimental import pallas as pl
from jax.experimental.pallas import tpu as pltpu
from jax.sharding import PartitionSpec as P

MESH = pl.DeviceIdType.MESH
SIDE = 4
CHUNK = 64


def kernel(
    sections,
    psi, left, right, ops, coupling, live, out,
    held, after, close, far, lcat, rbuf, ybuf, acc, relay, direct, comb, red, parts,
    local_sem, halo_send, halo_recv, share_send, share_recv, send1, recv1, sendc, recvc, send2, recv2,
):
    sec = lax.axis_index("sec")
    term = lax.axis_index("term")
    x, y = term % SIDE, term // SIDE
    core = sec % 2
    partner = sec + 1 - 2 * core
    distant = (sec + sections - 1 + 2 * core) % sections
    has_distant = jnp.logical_and(sec > 0, sec < sections - 1)

    def mirror(b):
        return b + core * (3 - 2 * b)

    near = (
        (y * SIDE + (x + 1) % SIDE, y * SIDE + (x + 3) % SIDE, y * SIDE + (x + 2) % SIDE),
        ((y + 1) % SIDE * SIDE + x, (y + 3) % SIDE * SIDE + x, (y + 2) % SIDE * SIDE + x),
    )
    place = (x, y)
    order = [mirror(b) for b in (2, 3, 1, 0)]

    def fetch(n, src, dst):
        copy = pltpu.make_async_copy(src, dst, local_sem.at[n])
        copy.start()
        return copy

    local = [fetch(0, psi, held.at[pl.ds(0, 4)]), fetch(1, right, rbuf)]
    lefts = [fetch(2 + c, left.at[:, order[c]], lcat.at[c]) for c in range(4)]

    def at_sec(other):
        return {"sec": other, "term": term}

    def at_term(other):
        return {"sec": sec, "term": other}

    barrier = pltpu.get_barrier_semaphore()
    pl.semaphore_signal(barrier, inc=1, device_id=at_sec(partner), device_id_type=MESH)

    @pl.when(has_distant)
    def _():
        pl.semaphore_signal(barrier, inc=1, device_id=at_sec(distant), device_id_type=MESH)

    for axis in range(2):
        for d in range(3):
            pl.semaphore_signal(barrier, inc=1, device_id=at_term(near[axis][d]), device_id_type=MESH)
    pl.semaphore_wait(barrier, 7 + has_distant.astype(jnp.int32))

    def halo(n, src, dst, other):
        return pltpu.make_async_remote_copy(
            src_ref=src, dst_ref=dst, send_sem=halo_send.at[n], recv_sem=halo_recv.at[n],
            device_id=at_sec(other), device_id_type=MESH,
        )

    mine = x + core * (y - x)
    theirs = y + core * (x - y)

    def piece(q):
        return (0, pl.ds(pl.multiple_of(q * 64, 64), 64))

    halos = [
        halo(0, psi.at[(mirror(0),) + piece(theirs)], close.at[piece(theirs)], distant),
        halo(1, psi.at[(mirror(1),) + piece(theirs)], far.at[piece(theirs)], distant),
        halo(2, psi.at[mirror(0), pl.ds(1, 3)], close.at[pl.ds(1, 3)], distant),
        halo(3, psi.at[mirror(1), pl.ds(1, 3)], far.at[pl.ds(1, 3)], distant),
        halo(4, psi.at[mirror(3)], held.at[4], partner),
        halo(5, psi.at[mirror(2)], after, partner),
    ]
    shares = [
        [
            pltpu.make_async_remote_copy(
                src_ref=block.at[piece(mine)], dst_ref=block.at[piece(mine)],
                send_sem=share_send.at[n, d], recv_sem=share_recv.at[n, d],
                device_id=at_term(near[0][d] + core * (near[1][d] - near[0][d])), device_id_type=MESH,
            )
            for d in range(3)
        ]
        for n, block in enumerate((close, far))
    ]

    @pl.when(has_distant)
    def _():
        for copy in halos[:3]:
            copy.start()

    halos[4].start()
    halos[5].start()

    def compute(c):
        s = order[c]
        for t in range(4):
            target = coupling[t, s]
            valid = target >= 0
            block = jnp.where(valid, target - sec * 4, 0)
            seen = mirror(block)
            own = jnp.logical_and(block >= 0, block < 4)
            index = jnp.where(own, block, 4)
            coef = [
                [jnp.where(valid, ops[t, k, j], 0.0).astype(jnp.bfloat16) for j in range(4)] for k in range(4)
            ]
            weights = rbuf[t]
            for r in range(0, 256, CHUNK):
                rows = pl.ds(r, CHUNK)
                source = []
                for j in range(4):
                    value = held[index, j, rows, :]
                    if c == 1:
                        value = jnp.where(seen == 5, after[j, rows, :], value)
                    if c >= 2:
                        value = jnp.where(seen == -1, close[j, rows, :], value)
                    if c == 3:
                        value = jnp.where(seen == -2, far[j, rows, :], value)
                    source.append(value)
                mixed = []
                for k in range(4):
                    total = coef[k][0] * source[0]
                    for j in range(1, 4):
                        total = total + coef[k][j] * source[j]
                    mixed.append(total)
                inner = jnp.dot(
                    jnp.concatenate(mixed, axis=0), weights, preferred_element_type=jnp.float32
                ).astype(jnp.bfloat16)
                for k in range(4):
                    ybuf[t, rows, pl.ds(256 * k, 256)] = inner[k * CHUNK : (k + 1) * CHUNK]
        for k in range(4):
            total = None
            for t in range(4):
                term_part = jnp.dot(
                    lcat[c, t], ybuf[t, :, pl.ds(256 * k, 256)], preferred_element_type=jnp.float32
                )
                total = term_part if total is None else total + term_part
            acc[c, k] = total.astype(jnp.bfloat16).reshape(SIDE, SIDE, 16, 256)

    pending = []
    copies = {}

    def send(src, dst, send_sem, recv_sem, axis, direction):
        copy = pltpu.make_async_remote_copy(
            src_ref=src, dst_ref=dst, send_sem=send_sem, recv_sem=recv_sem,
            device_id=at_term(near[axis][direction]), device_id_type=MESH,
        )
        copy.start()
        pending.append(copy)
        return copy

    def targets(axis):
        at = place[axis]
        return ((at + 1) % SIDE, (at + 3) % SIDE, (at + 2) % SIDE)

    def slab(c, h, d, at):
        return (c, 2 * h + d, slice(None), at) if h == 0 else (c, 2 * h + d, at)

    def first(c):
        g, i = c // 2, c % 2
        for h in range(2):
            goal = targets(h)
            for d in range(2):
                copies[0, c, h, d] = send(
                    acc.at[slab(c, h, d, goal[2])], relay.at[g, h, d, i],
                    send1.at[c, h, 0, d], recv1.at[c, h, 0, d], h, d,
                )
            for d in range(2):
                copies[1, c, h, d] = send(
                    acc.at[slab(c, h, 1 - d, goal[d])], direct.at[g, h, d, i],
                    send1.at[c, h, 1, d], recv1.at[c, h, 1, d], h, d,
                )

    def pass_on(g):
        blocks = pl.ds(2 * g, 2)
        for h in range(2):
            goal = targets(h)
            for d in range(2):
                for i in range(2):
                    copies[0, 2 * g + i, h, d].wait_recv()
                own = acc[slab(blocks, h, d, goal[d])].astype(jnp.float32)
                relay[g, h, d] = (relay[g, h, d].astype(jnp.float32) + own).astype(jnp.bfloat16)
                copies[2, g, h, d] = send(
                    relay.at[g, h, d], comb.at[g, h, d], sendc.at[g, h, d], recvc.at[g, h, d], h, d
                )

    def second(g):
        blocks = pl.ds(2 * g, 2)
        for h in range(2):
            for d in range(2):
                for i in range(2):
                    copies[1, 2 * g + i, h, 1 - d].wait_recv()
                copies[2, g, h, d].wait_recv()
                total = acc[slab(blocks, h, d, place[h])].astype(jnp.float32)
                total = total + direct[g, h, 1 - d].astype(jnp.float32) + comb[g, h, d].astype(jnp.float32)
                red[g, h, d] = total.astype(jnp.bfloat16)
            goal = targets(1 - h)
            for d in (2, 0, 1):
                copies[3, g, h, d] = send(
                    red.at[g, h, :, :, goal[d]], parts.at[g, h, d], send2.at[g, h, d], recv2.at[g, h, d], 1 - h, d
                )

    def sent():
        while pending:
            pending.pop().wait_send()

    row = term * 16 + lax.broadcasted_iota(jnp.int32, (2, 16, 256), 1)
    column = lax.broadcasted_iota(jnp.int32, (2, 16, 256), 2)
    furthest = jnp.maximum(row, column)

    def finish(g):
        for h in range(2):
            total = red[g, h, :, :, place[1 - h]].astype(jnp.float32)
            for d in range(3):
                copies[3, g, h, d].wait_recv()
                total = total + parts[g, h, d].astype(jnp.float32)
            for i in range(2):
                s = order[2 * g + i]
                out[s, pl.ds(2 * h, 2)] = jnp.where(furthest < live[s], total[:, i], 0.0).astype(jnp.bfloat16)

    for copy in local:
        copy.wait()
    halos[4].wait_recv()

    @pl.when(has_distant)
    def _():
        for n in range(2):
            halos[n].wait_recv()
            for copy in shares[n]:
                copy.start()
        halos[3].start()

    lefts[0].wait()
    compute(0)
    first(0)

    lefts[1].wait()
    halos[5].wait_recv()
    compute(1)
    first(1)

    @pl.when(has_distant)
    def _():
        halos[2].wait_recv()
        for copy in shares[0]:
            copy.wait_recv()

    lefts[2].wait()
    compute(2)
    first(2)
    pass_on(0)

    @pl.when(has_distant)
    def _():
        halos[3].wait_recv()
        for copy in shares[1]:
            copy.wait_recv()

    lefts[3].wait()
    compute(3)
    first(3)
    second(0)
    pass_on(1)
    second(1)

    @pl.when(has_distant)
    def _():
        for copy in halos[:4] + shares[0] + shares[1]:
            copy.wait_send()

    halos[4].wait_send()
    halos[5].wait_send()
    finish(0)
    finish(1)
    sent()


def on_device(psi, left_env, right_env, site_ops, coupling, live):
    sec_count, states, width, _ = psi.shape
    row_count = width // lax.axis_size("term")
    anywhere = pl.BlockSpec(memory_space=pl.ANY)
    scalars = pl.BlockSpec(memory_space=pltpu.SMEM)
    bf16 = jnp.bfloat16
    dma = pltpu.SemaphoreType.DMA
    return pl.pallas_call(
        functools.partial(kernel, lax.axis_size("sec")),
        out_shape=jax.ShapeDtypeStruct((sec_count, states, row_count, width), bf16),
        in_specs=[anywhere, anywhere, anywhere, scalars, scalars, scalars],
        out_specs=pl.BlockSpec(memory_space=pltpu.VMEM),
        scratch_shapes=[
            pltpu.VMEM((5, 4, 256, 256), bf16),
            pltpu.VMEM((4, 256, 256), bf16),
            pltpu.VMEM((4, 256, 256), bf16),
            pltpu.VMEM((4, 256, 256), bf16),
            pltpu.VMEM((4, 4, 256, 256), bf16),
            pltpu.VMEM((4, 256, 256), bf16),
            pltpu.VMEM((4, 256, 1024), bf16),
            pltpu.VMEM((4, 4, SIDE, SIDE, 16, 256), bf16),
            pltpu.VMEM((2, 2, 2, 2, SIDE, 16, 256), bf16),
            pltpu.VMEM((2, 2, 2, 2, SIDE, 16, 256), bf16),
            pltpu.VMEM((2, 2, 2, 2, SIDE, 16, 256), bf16),
            pltpu.VMEM((2, 2, 2, 2, SIDE, 16, 256), bf16),
            pltpu.VMEM((2, 2, 3, 2, 2, 16, 256), bf16),
            dma((6,)),
            dma((6,)),
            dma((6,)),
            dma((2, 3)),
            dma((2, 3)),
            dma((4, 2, 2, 2)),
            dma((4, 2, 2, 2)),
            dma((2, 2, 2)),
            dma((2, 2, 2)),
            dma((2, 2, 3)),
            dma((2, 2, 3)),
        ],
        compiler_params=pltpu.CompilerParams(
            collective_id=0, has_side_effects=True, vmem_limit_bytes=63 << 20
        ),
    )(psi, left_env, right_env, site_ops, coupling, live)


def solution(mesh):
    placed = (
        P("sec", None, None, None),
        P("term", "sec", None, None),
        P("term", None, None),
        P("term", None, None),
        P("term", "sec"),
        P("sec"),
    )
    return jax.shard_map(
        on_device,
        mesh=mesh,
        in_specs=placed,
        out_specs=P("sec", None, "term", None),
        check_vma=False,
    )
```

```python
import functools

import jax
import jax.numpy as jnp
from jax import lax
from jax.experimental import pallas as pl
from jax.experimental.pallas import tpu as pltpu
from jax.sharding import PartitionSpec as P

MESH = pl.DeviceIdType.MESH
SIDE = 4
CHUNK = 64


def kernel(
    sections,
    psi, left, right, ops, coupling, live, out,
    held, after, close, far, lcat, rbuf, ybuf, acc, relay, direct, comb, red, parts,
    local_sem, halo_send, halo_recv, share_send, share_recv, send1, recv1, sendc, recvc, send2, recv2,
):
    sec = lax.axis_index("sec")
    term = lax.axis_index("term")
    x, y = term % SIDE, term // SIDE
    core = sec % 2
    partner = sec + 1 - 2 * core
    distant = (sec + sections - 1 + 2 * core) % sections
    has_distant = jnp.logical_and(sec > 0, sec < sections - 1)

    def mirror(b):
        return b + core * (3 - 2 * b)

    near = (
        (y * SIDE + (x + 1) % SIDE, y * SIDE + (x + 3) % SIDE, y * SIDE + (x + 2) % SIDE),
        ((y + 1) % SIDE * SIDE + x, (y + 3) % SIDE * SIDE + x, (y + 2) % SIDE * SIDE + x),
    )
    place = (x, y)
    order = [mirror(b) for b in (2, 3, 1, 0)]

    def fetch(n, src, dst):
        copy = pltpu.make_async_copy(src, dst, local_sem.at[n])
        copy.start()
        return copy

    local = [fetch(0, psi, held.at[pl.ds(0, 4)]), fetch(1, right, rbuf)]
    lefts = [fetch(2 + c, left.at[:, order[c]], lcat.at[c]) for c in range(4)]

    def at_sec(other):
        return {"sec": other, "term": term}

    def at_term(other):
        return {"sec": sec, "term": other}

    barrier = pltpu.get_barrier_semaphore()
    pl.semaphore_signal(barrier, inc=1, device_id=at_sec(partner), device_id_type=MESH)

    @pl.when(has_distant)
    def _():
        pl.semaphore_signal(barrier, inc=1, device_id=at_sec(distant), device_id_type=MESH)

    for axis in range(2):
        for d in range(3):
            pl.semaphore_signal(barrier, inc=1, device_id=at_term(near[axis][d]), device_id_type=MESH)
    pl.semaphore_wait(barrier, 7 + has_distant.astype(jnp.int32))

    def halo(n, src, dst, other):
        return pltpu.make_async_remote_copy(
            src_ref=src, dst_ref=dst, send_sem=halo_send.at[n], recv_sem=halo_recv.at[n],
            device_id=at_sec(other), device_id_type=MESH,
        )

    mine = x + core * (y - x)
    theirs = y + core * (x - y)

    def piece(q):
        return (0, pl.ds(pl.multiple_of(q * 64, 64), 64))

    halos = [
        halo(0, psi.at[(mirror(0),) + piece(theirs)], close.at[piece(theirs)], distant),
        halo(1, psi.at[(mirror(1),) + piece(theirs)], far.at[piece(theirs)], distant),
        halo(2, psi.at[mirror(0), pl.ds(1, 3)], close.at[pl.ds(1, 3)], distant),
        halo(3, psi.at[mirror(1), pl.ds(1, 3)], far.at[pl.ds(1, 3)], distant),
        halo(4, psi.at[mirror(3)], held.at[4], partner),
        halo(5, psi.at[mirror(2)], after, partner),
    ]
    shares = [
        [
            pltpu.make_async_remote_copy(
                src_ref=block.at[piece(mine)], dst_ref=block.at[piece(mine)],
                send_sem=share_send.at[n, d], recv_sem=share_recv.at[n, d],
                device_id=at_term(near[0][d] + core * (near[1][d] - near[0][d])), device_id_type=MESH,
            )
            for d in range(3)
        ]
        for n, block in enumerate((close, far))
    ]

    @pl.when(has_distant)
    def _():
        for copy in halos[:3]:
            copy.start()

    halos[4].start()
    halos[5].start()

    def compute(c):
        s = order[c]
        for t in range(4):
            target = coupling[t, s]
            valid = target >= 0
            block = jnp.where(valid, target - sec * 4, 0)
            seen = mirror(block)
            own = jnp.logical_and(block >= 0, block < 4)
            index = jnp.where(own, block, 4)
            coef = [
                [jnp.where(valid, ops[t, k, j], 0.0).astype(jnp.bfloat16) for j in range(4)] for k in range(4)
            ]
            weights = rbuf[t]
            for r in range(0, 256, CHUNK):
                rows = pl.ds(r, CHUNK)
                source = []
                for j in range(4):
                    value = held[index, j, rows, :]
                    if c == 1:
                        value = jnp.where(seen == 5, after[j, rows, :], value)
                    if c >= 2:
                        value = jnp.where(seen == -1, close[j, rows, :], value)
                    if c == 3:
                        value = jnp.where(seen == -2, far[j, rows, :], value)
                    source.append(value)
                mixed = []
                for k in range(4):
                    total = coef[k][0] * source[0]
                    for j in range(1, 4):
                        total = total + coef[k][j] * source[j]
                    mixed.append(total)
                inner = jnp.dot(
                    jnp.concatenate(mixed, axis=0), weights, preferred_element_type=jnp.float32
                ).astype(jnp.bfloat16)
                for k in range(4):
                    ybuf[t, rows, pl.ds(256 * k, 256)] = inner[k * CHUNK : (k + 1) * CHUNK]
        for k in range(4):
            total = None
            for t in range(4):
                term_part = jnp.dot(
                    lcat[c, t], ybuf[t, :, pl.ds(256 * k, 256)], preferred_element_type=jnp.float32
                )
                total = term_part if total is None else total + term_part
            acc[c, k] = total.astype(jnp.bfloat16).reshape(SIDE, SIDE, 16, 256)
            if k % 2:
                first(c, k // 2)

    pending = []
    copies = {}

    def send(src, dst, send_sem, recv_sem, axis, direction):
        copy = pltpu.make_async_remote_copy(
            src_ref=src, dst_ref=dst, send_sem=send_sem, recv_sem=recv_sem,
            device_id=at_term(near[axis][direction]), device_id_type=MESH,
        )
        copy.start()
        pending.append(copy)
        return copy

    def targets(axis):
        at = place[axis]
        return ((at + 1) % SIDE, (at + 3) % SIDE, (at + 2) % SIDE)

    def slab(c, h, d, at):
        return (c, 2 * h + d, slice(None), at) if h == 0 else (c, 2 * h + d, at)

    def first(c, h):
        g, i = c // 2, c % 2
        goal = targets(h)
        for d in range(2):
            copies[0, c, h, d] = send(
                acc.at[slab(c, h, d, goal[2])], relay.at[g, h, d, i],
                send1.at[c, h, 0, d], recv1.at[c, h, 0, d], h, d,
            )
        for d in range(2):
            copies[1, c, h, d] = send(
                acc.at[slab(c, h, 1 - d, goal[d])], direct.at[g, h, d, i],
                send1.at[c, h, 1, d], recv1.at[c, h, 1, d], h, d,
            )

    def pass_on(g):
        blocks = pl.ds(2 * g, 2)
        for h in range(2):
            goal = targets(h)
            for d in range(2):
                for i in range(2):
                    copies[0, 2 * g + i, h, d].wait_recv()
                own = acc[slab(blocks, h, d, goal[d])].astype(jnp.float32)
                relay[g, h, d] = (relay[g, h, d].astype(jnp.float32) + own).astype(jnp.bfloat16)
                copies[2, g, h, d] = send(
                    relay.at[g, h, d], comb.at[g, h, d], sendc.at[g, h, d], recvc.at[g, h, d], h, d
                )

    def second(g):
        blocks = pl.ds(2 * g, 2)
        for h in range(2):
            for d in range(2):
                for i in range(2):
                    copies[1, 2 * g + i, h, 1 - d].wait_recv()
                copies[2, g, h, d].wait_recv()
                total = acc[slab(blocks, h, d, place[h])].astype(jnp.float32)
                total = total + direct[g, h, 1 - d].astype(jnp.float32) + comb[g, h, d].astype(jnp.float32)
                red[g, h, d] = total.astype(jnp.bfloat16)
            goal = targets(1 - h)
            for d in (2, 0, 1):
                copies[3, g, h, d] = send(
                    red.at[g, h, :, :, goal[d]], parts.at[g, h, d], send2.at[g, h, d], recv2.at[g, h, d], 1 - h, d
                )

    def sent():
        while pending:
            pending.pop().wait_send()

    row = term * 16 + lax.broadcasted_iota(jnp.int32, (2, 16, 256), 1)
    column = lax.broadcasted_iota(jnp.int32, (2, 16, 256), 2)
    furthest = jnp.maximum(row, column)

    def finish(g):
        for h in range(2):
            total = red[g, h, :, :, place[1 - h]].astype(jnp.float32)
            for d in range(3):
                copies[3, g, h, d].wait_recv()
                total = total + parts[g, h, d].astype(jnp.float32)
            for i in range(2):
                s = order[2 * g + i]
                out[s, pl.ds(2 * h, 2)] = jnp.where(furthest < live[s], total[:, i], 0.0).astype(jnp.bfloat16)

    for copy in local:
        copy.wait()
    halos[4].wait_recv()

    @pl.when(has_distant)
    def _():
        for n in range(2):
            halos[n].wait_recv()
            for copy in shares[n]:
                copy.start()
        halos[3].start()

    lefts[0].wait()
    compute(0)

    lefts[1].wait()
    halos[5].wait_recv()
    compute(1)

    @pl.when(has_distant)
    def _():
        halos[2].wait_recv()
        for copy in shares[0]:
            copy.wait_recv()

    lefts[2].wait()
    compute(2)
    pass_on(0)

    @pl.when(has_distant)
    def _():
        halos[3].wait_recv()
        for copy in shares[1]:
            copy.wait_recv()

    lefts[3].wait()
    compute(3)
    second(0)
    pass_on(1)
    second(1)

    @pl.when(has_distant)
    def _():
        for copy in halos[:4] + shares[0] + shares[1]:
            copy.wait_send()

    halos[4].wait_send()
    halos[5].wait_send()
    finish(0)
    finish(1)
    sent()


def on_device(psi, left_env, right_env, site_ops, coupling, live):
    sec_count, states, width, _ = psi.shape
    row_count = width // lax.axis_size("term")
    anywhere = pl.BlockSpec(memory_space=pl.ANY)
    scalars = pl.BlockSpec(memory_space=pltpu.SMEM)
    bf16 = jnp.bfloat16
    dma = pltpu.SemaphoreType.DMA
    return pl.pallas_call(
        functools.partial(kernel, lax.axis_size("sec")),
        out_shape=jax.ShapeDtypeStruct((sec_count, states, row_count, width), bf16),
        in_specs=[anywhere, anywhere, anywhere, scalars, scalars, scalars],
        out_specs=pl.BlockSpec(memory_space=pltpu.VMEM),
        scratch_shapes=[
            pltpu.VMEM((5, 4, 256, 256), bf16),
            pltpu.VMEM((4, 256, 256), bf16),
            pltpu.VMEM((4, 256, 256), bf16),
            pltpu.VMEM((4, 256, 256), bf16),
            pltpu.VMEM((4, 4, 256, 256), bf16),
            pltpu.VMEM((4, 256, 256), bf16),
            pltpu.VMEM((4, 256, 1024), bf16),
            pltpu.VMEM((4, 4, SIDE, SIDE, 16, 256), bf16),
            pltpu.VMEM((2, 2, 2, 2, SIDE, 16, 256), bf16),
            pltpu.VMEM((2, 2, 2, 2, SIDE, 16, 256), bf16),
            pltpu.VMEM((2, 2, 2, 2, SIDE, 16, 256), bf16),
            pltpu.VMEM((2, 2, 2, 2, SIDE, 16, 256), bf16),
            pltpu.VMEM((2, 2, 3, 2, 2, 16, 256), bf16),
            dma((6,)),
            dma((6,)),
            dma((6,)),
            dma((2, 3)),
            dma((2, 3)),
            dma((4, 2, 2, 2)),
            dma((4, 2, 2, 2)),
            dma((2, 2, 2)),
            dma((2, 2, 2)),
            dma((2, 2, 3)),
            dma((2, 2, 3)),
        ],
        compiler_params=pltpu.CompilerParams(
            collective_id=0, has_side_effects=True, vmem_limit_bytes=63 << 20
        ),
    )(psi, left_env, right_env, site_ops, coupling, live)


def solution(mesh):
    placed = (
        P("sec", None, None, None),
        P("term", "sec", None, None),
        P("term", None, None),
        P("term", None, None),
        P("term", "sec"),
        P("sec"),
    )
    return jax.shard_map(
        on_device,
        mesh=mesh,
        in_specs=placed,
        out_specs=P("sec", None, "term", None),
        check_vma=False,
    )
```
